256 devices in a mesh: seq: 64 (over z, y, core), tp: 4 (over x).
Axes of the slice: x: 4, y: 4, z: 8, core: 2. Of those that a mesh axis runs over, the one named last changes fastest.
Arguments:
- hidden_in: bfloat16 [1536, 8192], P('seq', 'tp'), may hold values from -8 to 8
- kv_weight: bfloat16 [8192, 1024], P('tp'), may hold values from -0.0625 to 0.0625
- queries: bfloat16 [1536, 4096], P('seq', 'tp'), may hold values from -15 to 15
- prefix_keys: bfloat16 [512, 128, 512], P('seq', None, 'tp'), may hold values from -6 to 6
- prefix_values: bfloat16 [512, 128, 512], P('seq', None, 'tp'), may hold values from -6 to 6
- page_table: int32 [512], replicated, may hold values from 0 to 511, each once
- suffix_lengths: int32 [2, 8], replicated, may hold values from 1 to 160, 768 in all within a row
- out_weight: bfloat16 [4096, 4096], P('tp'), may hold values from -0.09375 to 0.09375
Outputs:
- hidden: bfloat16 [1536, 4096], P('seq', 'tp')
- new_pages: bfloat16 [1536, 1024], P('seq', 'tp')
The draws below stay inside these ranges and needn't reach their ends.
Inputs may be any that keep to these rules, and one draw needn't show every extreme that they name: `page_table`: a permutation of the 512 cache pages; entries 256 * g to 256 * g + 255 are group g's prefix pages. `suffix_lengths`: each row sums to 768; group g's requests take its suffix tokens in order of their place u; some request has exactly 160 tokens.
All inputs are finite; a program needn't handle non-finite values.
Results may differ from the reference program's by a relative error of at most 0.0095.
Values may be sent and summed in bfloat16 or wider, within the bound.
A program may use at most 192 MiB of HBM per device.

```python
import math
import jax
import jax.numpy as jnp
import numpy as np
from jax import lax

D = 8192
DOUT = 4096
QH = 32
KVH = 4
HD = 128
PAGE = 128
GROUPS = 2
REQS = 8
S_DEV = 24
SUFFIX = 1536
HALF = 768
POOL = 512
GROUP_PAGES = 256
PREFIX = 32768
LMAX = 160


def draw_queries(key, part):
    noise_key = jax.random.fold_in(key, 11)
    full_shape = (SUFFIX, QH * HD)
    return (2.5 * jax.random.truncated_normal(noise_key, -6.0, 6.0, full_shape)).astype(jnp.bfloat16)


def draw_prefix_keys(key, part):
    noise_key = jax.random.fold_in(key, 23)
    full_shape = (POOL, PAGE, KVH * HD)
    return jax.random.truncated_normal(noise_key, -6.0, 6.0, full_shape).astype(jnp.bfloat16)


def block_scale(stream_key, dims, pieces, smallest, largest):
    level = 1.0
    for dim, shards_of in pieces:
        heights = jax.random.uniform(jax.random.fold_in(jax.random.fold_in(stream_key, 6), dim), (shards_of,), jnp.float32, smallest / len(pieces), largest / len(pieces))
        level = level * jnp.repeat(jnp.exp(heights), dims[dim] // shards_of).reshape((-1,) + (1,) * (len(dims) - 1 - dim))
    return level


def split_up(number_of, total, most, slope):
    weights = [(1 << 20) // math.isqrt(standing ** slope) + 1 for standing in range(2, number_of + 1)]
    rest, holding = total - most - (number_of - 1), [1] * (number_of - 1)
    while rest > 0:
        movable = [i for i in range(number_of - 1) if holding[i] < most]
        pool, left = sum([weights[i] for i in movable]), rest
        for i in movable:
            extra = min(most - holding[i], max(1, left * weights[i] // pool), rest)
            holding[i] = holding[i] + extra
            rest = rest - extra
    return np.array([most] + holding)


def ragged_sizes(stream_key, count, total, bound, skew):
    if count == 2:
        one = jax.random.randint(stream_key, (), max(1, total - bound), min(bound, total - 1) + 1)
        return jnp.stack([one, total - one])
    sizes = jnp.asarray(split_up(count, total, bound, skew), jnp.int32)
    twos = (count - 1) // 2
    donor, taker = sizes[1:1 + 2 * twos:2], sizes[2:2 + 2 * twos:2]
    slack = jnp.minimum(donor - 1, bound - taker)
    moved = jax.random.randint(jax.random.fold_in(stream_key, 1), (twos,), 0, 1 << 20) % (slack + 1)
    sizes = sizes.at[1:1 + 2 * twos:2].set(donor - moved).at[2:2 + 2 * twos:2].set(taker + moved)
    return sizes[jax.random.permutation(jax.random.fold_in(stream_key, 2), count)]


def gaussian(stream_key, extent, scale, most, cuts=(), kind=jnp.bfloat16):
    drawn = scale * jax.random.normal(stream_key, extent, jnp.float32)
    if cuts:
        drawn = drawn * block_scale(stream_key, extent, cuts, -0.22, 0.18)
    return jnp.clip(drawn, -most, most).astype(kind)


def setup_inputs(seed: int = 0) -> dict:
    streams_of = jax.random.split(jax.random.key(seed), 9)
    hidden_in = gaussian(streams_of[0], (SUFFIX, D), 1.6, 8.0, ((0, 64), (1, 4)))
    kv_weight = gaussian(streams_of[1], (D, KVH * 2 * HD), D ** -0.5, 0.0625, ((0, 4),))
    queries = draw_queries(jax.random.fold_in(streams_of[8], 71), 0)
    prefix_keys = draw_prefix_keys(jax.random.fold_in(streams_of[8], 71), 0)
    prefix_values = gaussian(streams_of[4], (POOL, PAGE, KVH * HD), 1.0, 6.0, ((0, 64), (2, 4)))
    page_table = jax.random.permutation(streams_of[5], POOL).astype(jnp.int32)
    suffix_lengths = jax.vmap(lambda own: ragged_sizes(own, REQS, HALF, LMAX, 2))(jax.random.split(streams_of[6], GROUPS)).reshape((GROUPS, REQS)).astype(jnp.int32)
    out_weight = gaussian(streams_of[7], (QH * HD, DOUT), (QH * HD) ** -0.5, 0.09375, ((0, 4),))
    return dict(hidden_in=hidden_in, kv_weight=kv_weight, queries=queries, prefix_keys=prefix_keys, prefix_values=prefix_values, page_table=page_table, suffix_lengths=suffix_lengths, out_weight=out_weight)


masked_score = -1e+30

def place_tokens(tokens, block_rows):
    blocks = tokens // block_rows
    groups = (blocks % GROUPS).astype(jnp.int32)
    within = (blocks // GROUPS * block_rows + tokens % block_rows).astype(jnp.int32)
    return (groups, within)

def token_table(groups, within, lengths):
    picker = (groups[:, None] == jnp.arange(GROUPS, dtype=jnp.int32)[None, :]).astype(jnp.int32)
    end_marks = jnp.cumsum(lengths, axis=1).astype(jnp.int32)
    token_ends = lax.optimization_barrier(jnp.sum(picker[:, :, None] * end_marks[None, :, :], axis=1))
    token_lens = lax.optimization_barrier(jnp.sum(picker[:, :, None] * lengths[None, :, :], axis=1))
    passed = (within[:, None] >= token_ends).astype(jnp.int32)
    request = lax.optimization_barrier(jnp.sum(passed, axis=1)).astype(jnp.int32)
    offset = (within - lax.optimization_barrier(jnp.sum(passed * token_lens, axis=1))).astype(jnp.int32)
    return (groups * REQS + request, offset)

def rotate(key_rows, positions):
    half_dim = HD // 2
    frequency = jnp.power(500000.0, -(jnp.arange(half_dim, dtype=jnp.float32) * 2.0 / HD))
    angles = positions.astype(jnp.float32)[:, None] * frequency[None, :]
    cosine = jnp.cos(angles)[:, None, :]
    sine_part = jnp.sin(angles)[:, None, :]
    leading = key_rows[..., :half_dim]
    trailing = key_rows[..., half_dim:]
    return jnp.concatenate([leading * cosine - trailing * sine_part, trailing * cosine + leading * sine_part], axis=-1)

def rounded(weights):
    narrow = lax.optimization_barrier(weights.astype(jnp.bfloat16))
    return narrow.astype(jnp.float32)

def reference(hidden_in, kv_weight, queries, prefix_keys, prefix_values, page_table, suffix_lengths, out_weight):
    tokens = jnp.arange(SUFFIX, dtype=jnp.int32)
    groups, within = place_tokens(tokens, S_DEV)
    request_ids, offsets = token_table(groups, within, suffix_lengths)
    projected = jnp.dot(hidden_in, kv_weight, preferred_element_type=jnp.float32).reshape(SUFFIX, KVH, 2, HD)
    rotated = rotate(projected[:, :, 0], PREFIX + offsets)
    new_pages = jnp.stack([rotated, projected[:, :, 1]], axis=2).reshape(SUFFIX, KVH * 2 * HD).astype(jnp.bfloat16)
    page_kv = new_pages.reshape(SUFFIX, KVH, 2, HD).astype(jnp.float32)
    page_rows = page_table.reshape(GROUPS, GROUP_PAGES)
    score_scale = 1.0 / math.sqrt(HD)
    group_q = QH // KVH
    highest = lax.Precision.HIGHEST
    places = jnp.arange(HALF, dtype=jnp.int32)

    def one_block(block_index):
        first_row = (block_index * S_DEV).astype(jnp.int32)
        group_index = (block_index % GROUPS).astype(jnp.int32)
        first_place = (block_index // GROUPS * S_DEV).astype(jnp.int32)
        query_block = lax.dynamic_slice_in_dim(queries, first_row, S_DEV, 0).astype(jnp.float32)
        query_block = query_block.reshape(S_DEV, KVH, group_q, HD)
        slot_ids = lax.dynamic_index_in_dim(page_rows, group_index, 0, keepdims=False)
        cache_keys = jnp.take(prefix_keys, slot_ids, axis=0).astype(jnp.float32).reshape(PREFIX, KVH, HD)
        cache_vals = jnp.take(prefix_values, slot_ids, axis=0).astype(jnp.float32).reshape(PREFIX, KVH, HD)
        prefix_scores = jnp.einsum('tkgd,pkd->tkgp', query_block, cache_keys, precision=highest) * score_scale
        group_tokens = (places // S_DEV * GROUPS + group_index) * S_DEV + places % S_DEV
        own_kv = jnp.take(page_kv, group_tokens, axis=0)
        own_ids = jnp.take(request_ids, group_tokens, axis=0)
        row_ids = lax.dynamic_slice_in_dim(request_ids, first_row, S_DEV, 0)
        row_pos = first_place + jnp.arange(S_DEV, dtype=jnp.int32)
        visible = (own_ids[None, :] == row_ids[:, None]) & (places[None, :] <= row_pos[:, None])
        suffix_scores = jnp.einsum('tkgd,pkd->tkgp', query_block, own_kv[:, :, 0], precision=highest) * score_scale
        suffix_scores = jnp.where(visible[:, None, None, :], suffix_scores, masked_score)
        row_top = jnp.maximum(lax.optimization_barrier(jnp.max(prefix_scores, axis=-1)), lax.optimization_barrier(jnp.max(suffix_scores, axis=-1)))
        prefix_weight = jnp.exp(prefix_scores - row_top[..., None])
        suffix_weight = jnp.exp(suffix_scores - row_top[..., None]) * visible[:, None, None, :].astype(jnp.float32)
        row_total = lax.optimization_barrier(jnp.sum(prefix_weight, axis=-1)) + lax.optimization_barrier(jnp.sum(suffix_weight, axis=-1))
        row_mix = jnp.einsum('tkgp,pkd->tkgd', rounded(prefix_weight), cache_vals, precision=highest)
        row_mix = row_mix + jnp.einsum('tkgp,pkd->tkgd', rounded(suffix_weight), own_kv[:, :, 1], precision=highest)
        return (row_mix / row_total[..., None]).reshape(S_DEV, QH * HD)
    attended = lax.map(one_block, jnp.arange(SUFFIX // S_DEV, dtype=jnp.int32))
    attended = attended.reshape(SUFFIX, QH * HD).astype(jnp.bfloat16)
    hidden = jnp.dot(attended, out_weight, preferred_element_type=jnp.float32).astype(jnp.bfloat16)
    return (hidden, new_pages)
```

```python
import functools
import math

import jax
import jax.numpy as jnp
import numpy as np
from jax import lax
from jax.experimental import pallas as pl
from jax.experimental.pallas import tpu as pltpu
from jax.sharding import PartitionSpec as P

HD = 128
PAGE = 128
GROUPS = 2
REQS = 8
NY = 4
TP = 4
T = 24
TW = 32
HEADS = 8
PAGES = 8
CHUNK = 4
CK = CHUNK * PAGE
NCH = PAGES // CHUNK
PREFIX = 32768
NEG = -1e30
LOG2E = 1.0 / math.log(2.0)
SCALE2 = LOG2E / math.sqrt(HD)
MSG = HEADS * HD + 128
BF = jnp.bfloat16
F32 = jnp.float32
NT = (((1,), (1,)), ((), ()))
TWO_PI = 2.0 * math.pi


def split_constant(value, bits):
    exponent = math.floor(math.log2(value))
    unit = 2.0 ** (exponent - bits)
    head = math.floor(value / unit) * unit
    return head, value - head


TURN_A, REST = split_constant(TWO_PI, 9)
TURN_B, REST = split_constant(REST, 9)
TURN_C = REST


def lane_iota(shape):
    return lax.broadcasted_iota(jnp.int32, shape, 1)


def row_iota(shape):
    return lax.broadcasted_iota(jnp.int32, shape, 0)


def packed_lse(lse):
    hi = lse.astype(BF).astype(F32)
    rest = lse - hi
    mid = rest.astype(BF).astype(F32)
    low = (rest - mid).astype(BF).astype(F32)
    lane = lane_iota(lse.shape)
    out = jnp.where(lane < 24, pltpu.roll(low, 16, 1), 0.0)
    out = jnp.where(lane < 16, pltpu.roll(mid, 8, 1), out)
    return jnp.where(lane < 8, hi, out).astype(BF)


def unpacked_lse(packed):
    terms = packed.astype(F32)
    return terms + pltpu.roll(terms, 120, 1) + pltpu.roll(terms, 112, 1)


def shares(lses):
    top = functools.reduce(jnp.maximum, lses)
    weights = [jnp.exp2(lse - top) for lse in lses]
    total = functools.reduce(jnp.add, weights)
    inverse = 1.0 / total
    return top, total, [w * inverse for w in weights]


def merged_head(parts, fractions, a):
    out = None
    for part, fraction in zip(parts, fractions):
        f = jnp.broadcast_to(fraction[:, a : a + 1], (T, HD))
        term = part(a) * f
        out = term if out is None else out + term
    return out


def head_of(msg):
    return lambda a: msg[:, a * HD : (a + 1) * HD].astype(F32)


def merge_messages(messages, store):
    lses = [unpacked_lse(m[:, HEADS * HD :]) for m in messages]
    top, total, fractions = shares(lses)
    parts = [head_of(m) for m in messages]
    for a in range(HEADS):
        store[:, a * HD : (a + 1) * HD] = merged_head(parts, fractions, a).astype(BF)
    store[:, HEADS * HD :] = packed_lse(top + jnp.log(total) * LOG2E)


def kernel(
    nz,
    hid_ref,
    kvw_hbm,
    q_ref,
    k_hbm,
    v_hbm,
    pt_ref,
    len_ref,
    freq_ref,
    ow_hbm,
    hidden_ref,
    pages_ref,
    kvw,
    ow,
    kbuf,
    vbuf,
    qbuf,
    qc,
    gmat,
    kp,
    vt,
    acc,
    stat,
    ot,
    st,
    msgs,
    half,
    fromup,
    fromdown,
    sendup,
    senddown,
    kvpart,
    kvin,
    win,
    osuf,
    lsuf,
    att,
    oown,
    osend,
    oin,
    wsem,
    ksend,
    vsend,
    krecv,
    vrecv,
    qsend,
    qrecv,
    q2send,
    q2recv,
    tsend,
    trecv,
    winsend,
    winrecv,
    hsend,
    hrecv,
    upsend,
    uprecv,
    downsend,
    downrecv,
    osendsem,
    orecvsem,
    localsem,
):
    s = lax.axis_index("seq")
    x = lax.axis_index("tp")
    z = s // (2 * NY)
    y = (s // 2) % NY
    c = s % 2
    ups = nz // 2
    downs = nz - 1 - ups

    def seq_at(zz, yy, cc):
        return {"seq": ((zz + nz) % nz * NY + (yy + NY) % NY) * 2 + cc}

    zup, zdown = seq_at(z + 1, y, c), seq_at(z - 1, y, c)
    yup, ydown, yfar = seq_at(z, y + 1, c), seq_at(z, y - 1, c), seq_at(z, y + 2, c)
    other = seq_at(z, y, 1 - c)
    yu, yd, yf = (y + 1) % NY, (y + NY - 1) % NY, (y + 2) % NY

    def remote(src, dst, send, recv, device):
        return pltpu.make_async_remote_copy(
            src_ref=src,
            dst_ref=dst,
            send_sem=send,
            recv_sem=recv,
            device_id=device,
            device_id_type=pl.DeviceIdType.MESH,
        )

    def arrived(ref, sem):
        pltpu.make_async_copy(ref, ref, sem).wait()

    barrier = pltpu.get_barrier_semaphore()
    peers = [zup, zdown, yup, ydown, yfar, other] + [{"tp": (x + i) % TP} for i in range(1, TP)]
    for peer in peers:
        pl.semaphore_signal(barrier, inc=1, device_id=peer, device_id_type=pl.DeviceIdType.MESH)

    own_k = pltpu.make_async_copy(k_hbm, kbuf.at[y], localsem.at[0])
    own_v = pltpu.make_async_copy(v_hbm, vbuf.at[y], localsem.at[1])
    own_q = pltpu.make_async_copy(q_ref, qbuf.at[c, z], localsem.at[2])
    load_kvw = pltpu.make_async_copy(kvw_hbm, kvw, localsem.at[3])
    own_k.start()
    own_v.start()
    own_q.start()
    load_kvw.start()
    load_ow = []
    for i in range(TP):
        target = (x + (2, 1, 3, 0)[i]) % TP
        cols = pl.ds(pl.multiple_of(target * 1024, 1024), 1024)
        load_ow.append(pltpu.make_async_copy(ow_hbm.at[:, cols], ow.at[i], wsem.at[i]))
        load_ow[i].start()
    own_k.wait()
    own_v.wait()
    own_q.wait()
    pl.semaphore_wait(barrier, len(peers))

    sent = []

    def go(copy):
        copy.start()
        sent.append(copy)

    def pass_query(block, step, up):
        device, slot = (zup, step) if up else (zdown, ups + step)
        ref = qbuf.at[c, block]
        go(remote(ref, ref, qsend.at[slot], qrecv.at[block], device))

    def share_query(block):
        ref = qbuf.at[c, block]
        go(remote(ref, ref, q2send.at[block], q2recv.at[block], other))

    pass_query(z, 0, True)
    if downs:
        pass_query(z, 0, False)

    def pages_of(ref, owner, ch):
        return ref.at[owner, pl.ds(ch * CHUNK, CHUNK)]

    for first, second in ((True, False), (False, True)):
        for ch in range(NCH):
            for is_k, device, way in ((first, yup, 0), (second, ydown, 1)):
                buf, ss, rs = (kbuf, ksend, krecv) if is_k else (vbuf, vsend, vrecv)
                ref = pages_of(buf, y, ch)
                go(remote(ref, ref, ss.at[way, ch], rs.at[y, ch], device))
    share_query(z)

    page_row = lax.broadcasted_iota(jnp.int32, (NY * PAGES, 1), 0)
    page_ids = ((z * NY + page_row // PAGES) * 2 + c) * PAGES + page_row % PAGES
    table = pt_ref[...]
    owner = (lane_iota(table.shape) // (table.shape[1] // GROUPS)).astype(F32)
    group_col = jnp.sum(jnp.where(table == page_ids, owner, 0.0), axis=1, keepdims=True)
    gmat[...] = jnp.broadcast_to(group_col, gmat.shape)

    load_kvw.wait()
    for h in range(TP):
        kvpart[h] = jnp.dot(
            hid_ref[...], kvw[:, h * 256 : (h + 1) * 256], preferred_element_type=F32
        )
    for i in (2, 1, 3):
        target = (x + i) % TP
        go(remote(kvpart.at[target], kvin.at[x], tsend.at[i], trecv.at[x], {"tp": target}))

    def query_step(step):
        if step < ups:
            block = (z + nz - 1 - step) % nz
            arrived(qbuf.at[c, block], qrecv.at[block])
            if step + 1 < ups:
                pass_query(block, step + 1, True)
            share_query(block)
        if step < downs:
            block = (z + 1 + step) % nz
            arrived(qbuf.at[c, block], qrecv.at[block])
            if step + 1 < downs:
                pass_query(block, step + 1, False)
            share_query(block)

    query_step(0)

    token = row_iota((T, 1))
    place = (z * NY + y) * T + token
    end = 0
    before = jnp.zeros((T, 1), jnp.int32)
    for r in range(REQS):
        size = len_ref[c, r]
        end = end + size
        before = before + jnp.where(place >= end, size, 0)
    offset = place - before
    position = (PREFIX + offset).astype(F32)
    angle = position * freq_ref[...]
    turns = jnp.floor(angle * (1.0 / TWO_PI) + 0.5)
    reduced = ((angle - turns * TURN_A) - turns * TURN_B) - turns * TURN_C
    cosine = jnp.cos(reduced)
    sine = jnp.sin(reduced)
    sine = jnp.where(lane_iota((T, HD)) < HD // 2, -sine, sine)

    if nz > 2:
        query_step(1)

    total = kvpart[x]
    for i in (1, 3, 2):
        source = (x + i) % TP
        arrived(kvin.at[source], trecv.at[source])
        total = total + kvin[source]
    key, value = total[:, :HD], total[:, HD:]
    rotated = key * cosine + pltpu.roll(key, HD // 2, 1) * sine
    fresh = jnp.concatenate([rotated, value], axis=1)
    pages_ref[...] = fresh.astype(BF)
    win[2, y] = jnp.concatenate([fresh, jnp.zeros((TW - T, 2 * HD), F32)], axis=0).astype(BF)
    mine = win.at[2, y]
    go(remote(mine, mine, winsend.at[0], winrecv.at[y], yup))
    go(remote(mine, mine, winsend.at[1], winrecv.at[y], ydown))
    go(remote(mine, mine, winsend.at[2], winrecv.at[y], yfar))

    for step in range(2, ups):
        query_step(step)

    for source in (yu, yd, yf):
        arrived(win.at[2, source], winrecv.at[source])
    go(remote(win.at[2], win.at[1], winsend.at[3], winrecv.at[NY], zup))

    for i in range(nz):
        arrived(qbuf.at[1 - c, i], q2recv.at[i])
    for zp in range(nz // 2):
        for a in range(HEADS):
            for g in range(GROUPS):
                pair = [
                    qbuf[g, 2 * zp + i, :, a * HD : (a + 1) * HD].astype(F32) for i in range(2)
                ]
                qc[pl.ds(a * nz * T + zp * 2 * T, 2 * T), g * HD : (g + 1) * HD] = (
                    jnp.concatenate(pair, axis=0).astype(BF)
                )

    tiles = HEADS * nz * T // 256
    acc[...] = jnp.zeros_like(acc)
    stat[...] = jnp.where(lax.broadcasted_iota(jnp.int32, stat.shape, 1) < 2, NEG, 0.0)

    def attend(owner_y, ch):
        gates = []
        for j in range(CHUNK):
            page = ch * CHUNK + j
            gate = gmat[pl.ds(owner_y * PAGES + page, 1), :]
            gates.append(gate)
            g1 = gate[:, :HD]
            keys = kbuf[owner_y, page].astype(F32)
            kp[j * PAGE : (j + 1) * PAGE, :] = jnp.concatenate(
                [keys * (1.0 - g1), keys * g1], axis=1
            ).astype(BF)
            vals = vbuf[owner_y, page].astype(F32).T
            vt[:HD, j * PAGE : (j + 1) * PAGE] = (vals * (1.0 - g1)).astype(BF)
            vt[HD:, j * PAGE : (j + 1) * PAGE] = (vals * g1).astype(BF)
        for r in range(tiles):
            scores = lax.dot_general(
                kp[...], qc[r * 256 : (r + 1) * 256, :], NT, preferred_element_type=F32
            )
            parts = [scores[j * PAGE : (j + 1) * PAGE, :] * SCALE2 for j in range(CHUNK)]
            old0, old1 = stat[r, 0:1, :], stat[r, 1:2, :]
            new0, new1 = old0, old1
            for j in range(CHUNK):
                top = jnp.max(parts[j], axis=0, keepdims=True)
                new0 = jnp.maximum(new0, jnp.where(gates[j] > 0.5, NEG, top))
                new1 = jnp.maximum(new1, jnp.where(gates[j] > 0.5, top, NEG))
            fall0, fall1 = jnp.exp2(old0 - new0), jnp.exp2(old1 - new1)
            sum0, sum1 = stat[r, 2:3, :] * fall0, stat[r, 3:4, :] * fall1
            weights = []
            for j in range(CHUNK):
                w = jnp.exp2(parts[j] - jnp.where(gates[j] > 0.5, new1, new0))
                row = jnp.sum(w, axis=0, keepdims=True)
                sum0 = sum0 + jnp.where(gates[j] > 0.5, 0.0, row)
                sum1 = sum1 + jnp.where(gates[j] > 0.5, row, 0.0)
                weights.append(w.astype(BF))
            mixed = jnp.dot(
                vt[...], jnp.concatenate(weights, axis=0), preferred_element_type=F32
            )
            acc[r, :HD, :] = acc[r, :HD, :] * fall0 + mixed[:HD]
            acc[r, HD:, :] = acc[r, HD:, :] * fall1 + mixed[HD:]
            stat[r, 0:1, :] = new0
            stat[r, 1:2, :] = new1
            stat[r, 2:3, :] = sum0
            stat[r, 3:4, :] = sum1

    def forward_pages():
        for ch in range(NCH):
            ref = pages_of(kbuf, yd, ch)
            arrived(ref, krecv.at[yd, ch])
            go(remote(ref, ref, ksend.at[2, ch], krecv.at[yd, ch], yup))
            ref = pages_of(vbuf, yu, ch)
            arrived(ref, vrecv.at[yu, ch])
            go(remote(ref, ref, vsend.at[2, ch], vrecv.at[yu, ch], ydown))

    forward_pages()

    def step(i, carry):
        turn, ch = i // NCH, i % NCH
        owner_y = (y + turn + turn // 2 + (turn // 3) * (NY - 2)) % NY

        @pl.when(turn == 1)
        def _():
            arrived(pages_of(kbuf, yu, ch), krecv.at[yu, ch])

        @pl.when(turn == 2)
        def _():
            arrived(pages_of(vbuf, yd, ch), vrecv.at[yd, ch])

        @pl.when(turn == 3)
        def _():
            arrived(pages_of(kbuf, yf, ch), krecv.at[yf, ch])
            arrived(pages_of(vbuf, yf, ch), vrecv.at[yf, ch])

        attend(owner_y, ch)
        return carry

    def suffix():
        arrived(win.at[1], winrecv.at[NY])
        go(remote(win.at[1], win.at[0], winsend.at[4], winrecv.at[NY + 1], zup))
        arrived(win.at[0], winrecv.at[NY + 1])
        count = 3 * NY * TW
        key_lane = lane_iota((T, count))
        key_z = z - 2 + key_lane // (NY * TW)
        key_place = (key_z * NY + key_lane // TW % NY) * T + key_lane % TW
        seen = (
            (key_lane % TW < T) & (key_place >= 0) & (key_place <= place)
            & (key_place >= place - offset)
        )
        rows = [win[r, b] for r in range(3) for b in range(NY)]
        keys = jnp.concatenate([b[:, :HD] for b in rows], axis=0)
        vals = jnp.concatenate([b[:, HD:] for b in rows], axis=0)
        lse = jnp.zeros((T, HD), F32)
        for a in range(HEADS):
            sc = lax.dot_general(
                q_ref[:, a * HD : (a + 1) * HD], keys, NT, preferred_element_type=F32
            )
            sc = jnp.where(seen, sc * SCALE2, NEG)
            top = jnp.max(sc, axis=1, keepdims=True)
            w = jnp.where(seen, jnp.exp2(sc - top), 0.0)
            tot = jnp.sum(w, axis=1, keepdims=True)
            out = jnp.dot(w.astype(BF), vals, preferred_element_type=F32)
            osuf[:, a * HD : (a + 1) * HD] = out / tot
            lse = jnp.where(lane_iota((T, HD)) == a, top + jnp.log(tot) * LOG2E, lse)
        lsuf[...] = lse

    lax.fori_loop(0, NCH, step, 0)
    suffix()
    lax.fori_loop(NCH, NY * NCH, step, 0)

    for r in range(tiles):
        rows = pl.ds(r * 256, 256)
        s0, s1 = stat[r, 2:3, :], stat[r, 3:4, :]
        ok0, ok1 = s0 > 0.0, s1 > 0.0
        safe0, safe1 = jnp.where(ok0, s0, 1.0), jnp.where(ok1, s1, 1.0)
        inv0, inv1 = 1.0 / safe0, 1.0 / safe1
        lse0 = jnp.where(ok0, stat[r, 0:1, :] + jnp.log(safe0) * LOG2E, NEG)
        lse1 = jnp.where(ok1, stat[r, 1:2, :] + jnp.log(safe1) * LOG2E, NEG)
        ot[rows, :HD] = (acc[r, :HD, :] * inv0).T
        ot[rows, HD:] = (acc[r, HD:, :] * inv1).T
        st[rows, :] = jnp.where(row_iota((HD, 256)) == 0, lse0, lse1).T

    lane = lane_iota((T, HD))

    def build(block, g):
        lse = jnp.zeros((T, HD), F32)
        for a in range(HEADS):
            rows = pl.ds(pl.multiple_of(a * nz * T + block * T, 8), T)
            msgs[g, block, :, a * HD : (a + 1) * HD] = ot[rows, g * HD : (g + 1) * HD].astype(BF)
            col = jnp.broadcast_to(st[rows, g : g + 1], (T, HD))
            lse = jnp.where(lane == a, col, lse)
        msgs[g, block, :, HEADS * HD :] = packed_lse(lse)

    order = []
    for t in range(ups):
        order.append((z + ups - t) % nz)
        if t < downs:
            order.append((z + nz - downs + t) % nz)
    order.append(z)

    for i in range(nz):
        block = order[i]
        for g in range(GROUPS):
            @pl.when(c != g)
            def _():
                build(block, g)
        ref = msgs.at[1 - c, block]
        go(remote(ref, half.at[block], hsend.at[block], hrecv.at[block], other))
    for i in range(nz):
        block = order[i]
        for g in range(GROUPS):
            @pl.when(c == g)
            def _():
                build(block, g)

    def both(block):
        arrived(half.at[block], hrecv.at[block])
        return [msgs[c, block], half[block]]

    for t in range(ups):
        block = (z + ups - t) % nz
        parts = both(block)
        if t:
            arrived(fromup.at[t - 1], uprecv.at[t - 1])
            parts.append(fromup[t - 1])
        merge_messages(parts, sendup.at[t])
        go(remote(sendup.at[t], fromup.at[t], upsend.at[t], uprecv.at[t], zup))
        if t < downs:
            block = (z + nz - downs + t) % nz
            parts = both(block)
            if t:
                arrived(fromdown.at[t - 1], downrecv.at[t - 1])
                parts.append(fromdown[t - 1])
            merge_messages(parts, senddown.at[t])
            go(remote(senddown.at[t], fromdown.at[t], downsend.at[t], downrecv.at[t], zdown))
    last = both(z)
    arrived(fromup.at[ups - 1], uprecv.at[ups - 1])
    last.append(fromup[ups - 1])
    if downs:
        arrived(fromdown.at[downs - 1], downrecv.at[downs - 1])
        last.append(fromdown[downs - 1])
    top, total, fractions = shares(
        [unpacked_lse(m[:, HEADS * HD :]) for m in last] + [lsuf[...]]
    )
    parts = [head_of(m) for m in last] + [lambda a: osuf[:, a * HD : (a + 1) * HD]]
    for a in range(HEADS):
        att[:, a * HD : (a + 1) * HD] = merged_head(parts, fractions, a).astype(BF)

    for i in range(TP):
        load_ow[i].wait()
        partial = jnp.dot(att[...], ow[i], preferred_element_type=F32)
        if i < TP - 1:
            target = (x + (2, 1, 3)[i]) % TP
            osend[i] = partial.astype(BF)
            go(remote(osend.at[i], oin.at[x], osendsem.at[i], orecvsem.at[x], {"tp": target}))
        else:
            oown[...] = partial
    total = oown[...]
    for i in (1, 3, 2):
        source = (x + i) % TP
        arrived(oin.at[source], orecvsem.at[source])
        total = total + oin[source].astype(F32)
    hidden_ref[...] = total.astype(BF)

    for copy in sent:
        copy.wait_send()


def local(
    hidden_in, kv_weight, queries, prefix_keys, prefix_values, page_table, suffix_lengths, out_weight
):
    nz = lax.axis_size("seq") // (2 * NY)
    ups = nz // 2
    downs = max(nz - 1 - ups, 1)
    tiles = HEADS * nz * T // 256
    rows = HEADS * nz * T
    exponent = np.tile(np.arange(HD // 2) * 2.0 / HD, 2)
    freq = (500000.0 ** -exponent).astype(np.float32).reshape(1, HD)
    vmem = pl.BlockSpec(memory_space=pltpu.VMEM)
    anywhere = pl.BlockSpec(memory_space=pl.ANY)
    smem = pl.BlockSpec(memory_space=pltpu.SMEM)
    dma = pltpu.SemaphoreType.DMA
    pages = (NY, PAGES, PAGE, HD)
    scratch = [
        pltpu.VMEM((2048, 1024), BF),
        pltpu.VMEM((TP, 1024, 1024), BF),
        pltpu.VMEM(pages, BF),
        pltpu.VMEM(pages, BF),
        pltpu.VMEM((GROUPS, nz, T, HEADS * HD), BF),
        pltpu.VMEM((rows, GROUPS * HD), BF),
        pltpu.VMEM((NY * PAGES, 256), F32),
        pltpu.VMEM((CK, GROUPS * HD), BF),
        pltpu.VMEM((GROUPS * HD, CK), BF),
        pltpu.VMEM((tiles, GROUPS * HD, 256), F32),
        pltpu.VMEM((tiles, 8, 256), F32),
        pltpu.VMEM((rows, GROUPS * HD), F32),
        pltpu.VMEM((rows, HD), F32),
        pltpu.VMEM((GROUPS, nz, T, MSG), BF),
        pltpu.VMEM((nz, T, MSG), BF),
        pltpu.VMEM((ups, T, MSG), BF),
        pltpu.VMEM((downs, T, MSG), BF),
        pltpu.VMEM((ups, T, MSG), BF),
        pltpu.VMEM((downs, T, MSG), BF),
        pltpu.VMEM((TP, T, 2 * HD), F32),
        pltpu.VMEM((TP, T, 2 * HD), F32),
        pltpu.VMEM((3, NY, TW, 2 * HD), BF),
        pltpu.VMEM((T, HEADS * HD), F32),
        pltpu.VMEM((T, HD), F32),
        pltpu.VMEM((T, HEADS * HD), BF),
        pltpu.VMEM((T, 1024), F32),
        pltpu.VMEM((TP - 1, T, 1024), BF),
        pltpu.VMEM((TP, T, 1024), BF),
        dma((TP,)),
        dma((3, NCH)),
        dma((3, NCH)),
        dma((NY, NCH)),
        dma((NY, NCH)),
        dma((nz,)),
        dma((nz,)),
        dma((nz,)),
        dma((nz,)),
        dma((TP,)),
        dma((TP,)),
        dma((5,)),
        dma((NY + 2,)),
        dma((nz,)),
        dma((nz,)),
        dma((ups,)),
        dma((ups,)),
        dma((downs,)),
        dma((downs,)),
        dma((TP,)),
        dma((TP,)),
        dma((4,)),
    ]
    return pl.pallas_call(
        functools.partial(kernel, nz),
        out_shape=(
            jax.ShapeDtypeStruct((T, 1024), BF),
            jax.ShapeDtypeStruct((T, 2 * HD), BF),
        ),
        in_specs=[vmem, anywhere, vmem, anywhere, anywhere, vmem, smem, vmem, anywhere],
        out_specs=(vmem, vmem),
        scratch_shapes=scratch,
        compiler_params=pltpu.CompilerParams(
            collective_id=0, has_side_effects=True, vmem_limit_bytes=56 * 1024 * 1024
        ),
    )(
        hidden_in,
        kv_weight,
        queries,
        prefix_keys,
        prefix_values,
        page_table.reshape(1, -1),
        suffix_lengths,
        freq,
        out_weight,
    )


def solution(mesh):
    return jax.shard_map(
        local,
        mesh=mesh,
        in_specs=(
            P("seq", "tp"),
            P("tp", None),
            P("seq", "tp"),
            P("seq", None, "tp"),
            P("seq", None, "tp"),
            P(),
            P(),
            P("tp", None),
        ),
        out_specs=(P("seq", "tp"), P("seq", "tp")),
        check_vma=False,
    )
```

```python
import functools
import math

import jax
import jax.numpy as jnp
import numpy as np
from jax import lax
from jax.experimental import pallas as pl
from jax.experimental.pallas import tpu as pltpu
from jax.sharding import PartitionSpec as P

HD = 128
PAGE = 128
GROUPS = 2
REQS = 8
NY = 4
TP = 4
T = 24
TW = 32
HEADS = 8
PAGES = 8
CHUNK = 4
CK = CHUNK * PAGE
NCH = PAGES // CHUNK
PREFIX = 32768
NEG = -1e30
LOG2E = 1.0 / math.log(2.0)
SCALE2 = LOG2E / math.sqrt(HD)
MSG = HEADS * HD + 128
HALVES = ((4, 3, 5, 6), (2, 1, 7, 0))
NEAR_FIRST = (1, 7, 2, 6, 3, 5, 4)
BF = jnp.bfloat16
F32 = jnp.float32
NT = (((1,), (1,)), ((), ()))
TWO_PI = 2.0 * math.pi


def split_constant(value, bits):
    exponent = math.floor(math.log2(value))
    unit = 2.0 ** (exponent - bits)
    head = math.floor(value / unit) * unit
    return head, value - head


TURN_A, REST = split_constant(TWO_PI, 9)
TURN_B, REST = split_constant(REST, 9)
TURN_C = REST


def lane_iota(shape):
    return lax.broadcasted_iota(jnp.int32, shape, 1)


def row_iota(shape):
    return lax.broadcasted_iota(jnp.int32, shape, 0)


def packed_lse(lse):
    hi = lse.astype(BF).astype(F32)
    rest = lse - hi
    mid = rest.astype(BF).astype(F32)
    low = (rest - mid).astype(BF).astype(F32)
    lane = lane_iota(lse.shape)
    out = jnp.where(lane < 24, pltpu.roll(low, 16, 1), 0.0)
    out = jnp.where(lane < 16, pltpu.roll(mid, 8, 1), out)
    return jnp.where(lane < 8, hi, out).astype(BF)


def unpacked_lse(packed):
    terms = packed.astype(F32)
    return terms + pltpu.roll(terms, 120, 1) + pltpu.roll(terms, 112, 1)


def shares(lses):
    top = functools.reduce(jnp.maximum, lses)
    weights = [jnp.exp2(lse - top) for lse in lses]
    total = functools.reduce(jnp.add, weights)
    inverse = 1.0 / total
    return top, total, [w * inverse for w in weights]


def merged_head(parts, fractions, a):
    out = None
    for part, fraction in zip(parts, fractions):
        f = jnp.broadcast_to(fraction[:, a : a + 1], (T, HD))
        term = part(a) * f
        out = term if out is None else out + term
    return out


def head_of(msg):
    return lambda a: msg[:, a * HD : (a + 1) * HD].astype(F32)


def merge_messages(messages, store):
    lses = [unpacked_lse(m[:, HEADS * HD :]) for m in messages]
    top, total, fractions = shares(lses)
    parts = [head_of(m) for m in messages]
    for a in range(HEADS):
        store[:, a * HD : (a + 1) * HD] = merged_head(parts, fractions, a).astype(BF)
    store[:, HEADS * HD :] = packed_lse(top + jnp.log(total) * LOG2E)


def kernel(
    nz,
    hid_ref,
    kvw_hbm,
    q_ref,
    k_hbm,
    v_hbm,
    pt_ref,
    len_ref,
    freq_ref,
    ow_hbm,
    hidden_ref,
    pages_ref,
    kvw,
    ow,
    kbuf,
    vbuf,
    qbuf,
    qc,
    gmat,
    kp,
    vt,
    acc,
    stat,
    ot,
    st,
    msgs,
    half,
    inbox,
    outbox,
    kvpart,
    kvin,
    win,
    osuf,
    lsuf,
    att,
    oown,
    osend,
    oin,
    wsem,
    ksend,
    vsend,
    krecv,
    vrecv,
    qsend,
    qrecv,
    q2send,
    q2recv,
    tsend,
    trecv,
    winsend,
    winrecv,
    hsend,
    hrecv,
    isend,
    irecv,
    osendsem,
    orecvsem,
    localsem,
):
    s = lax.axis_index("seq")
    x = lax.axis_index("tp")
    z = s // (2 * NY)
    y = (s // 2) % NY
    c = s % 2
    def seq_at(zz, yy, cc):
        return {"seq": ((zz + nz) % nz * NY + (yy + NY) % NY) * 2 + cc}

    zup = seq_at(z + 1, y, c)
    yup, ydown, yfar = seq_at(z, y + 1, c), seq_at(z, y - 1, c), seq_at(z, y + 2, c)
    other = seq_at(z, y, 1 - c)
    yu, yd, yf = (y + 1) % NY, (y + NY - 1) % NY, (y + 2) % NY

    def remote(src, dst, send, recv, device):
        return pltpu.make_async_remote_copy(
            src_ref=src,
            dst_ref=dst,
            send_sem=send,
            recv_sem=recv,
            device_id=device,
            device_id_type=pl.DeviceIdType.MESH,
        )

    def arrived(ref, sem):
        pltpu.make_async_copy(ref, ref, sem).wait()

    barrier = pltpu.get_barrier_semaphore()
    peers = [seq_at(z + i, y, c) for i in NEAR_FIRST] + [yup, ydown, yfar, other]
    peers += [{"tp": (x + i) % TP} for i in range(1, TP)]
    for peer in peers:
        pl.semaphore_signal(barrier, inc=1, device_id=peer, device_id_type=pl.DeviceIdType.MESH)

    own_k = pltpu.make_async_copy(k_hbm, kbuf.at[y], localsem.at[0])
    own_v = pltpu.make_async_copy(v_hbm, vbuf.at[y], localsem.at[1])
    own_q = pltpu.make_async_copy(q_ref, qbuf.at[c, z], localsem.at[2])
    load_kvw = pltpu.make_async_copy(kvw_hbm, kvw, localsem.at[3])
    own_k.start()
    own_v.start()
    own_q.start()
    load_kvw.start()
    load_ow = []
    for i in range(TP):
        target = (x + (2, 1, 3, 0)[i]) % TP
        cols = pl.ds(pl.multiple_of(target * 1024, 1024), 1024)
        load_ow.append(pltpu.make_async_copy(ow_hbm.at[:, cols], ow.at[i], wsem.at[i]))
        load_ow[i].start()

    page_row = lax.broadcasted_iota(jnp.int32, (NY * PAGES, 1), 0)
    page_ids = ((z * NY + page_row // PAGES) * 2 + c) * PAGES + page_row % PAGES
    table = pt_ref[...]
    owner = (lane_iota(table.shape) // (table.shape[1] // GROUPS)).astype(F32)
    group_col = jnp.sum(jnp.where(table == page_ids, owner, 0.0), axis=1, keepdims=True)
    gmat[...] = jnp.broadcast_to(group_col, gmat.shape)

    token = row_iota((T, 1))
    place = (z * NY + y) * T + token
    end = 0
    before = jnp.zeros((T, 1), jnp.int32)
    for r in range(REQS):
        size = len_ref[c, r]
        end = end + size
        before = before + jnp.where(place >= end, size, 0)
    offset = place - before
    position = (PREFIX + offset).astype(F32)
    angle = position * freq_ref[...]
    turns = jnp.floor(angle * (1.0 / TWO_PI) + 0.5)
    reduced = ((angle - turns * TURN_A) - turns * TURN_B) - turns * TURN_C
    cosine = jnp.cos(reduced)
    sine = jnp.sin(reduced)
    sine = jnp.where(lane_iota((T, HD)) < HD // 2, -sine, sine)

    load_kvw.wait()
    for h in range(TP):
        kvpart[h] = jnp.dot(
            hid_ref[...], kvw[:, h * 256 : (h + 1) * 256], preferred_element_type=F32
        )

    tiles = HEADS * nz * T // 256
    acc[...] = jnp.zeros_like(acc)
    stat[...] = jnp.where(lax.broadcasted_iota(jnp.int32, stat.shape, 1) < 2, NEG, 0.0)
    own_k.wait()
    own_v.wait()
    own_q.wait()
    pl.semaphore_wait(barrier, len(peers))

    sent = []

    def go(copy):
        copy.start()
        sent.append(copy)

    def share_query(block):
        ref = qbuf.at[c, block]
        go(remote(ref, ref, q2send.at[block], q2recv.at[block], other))

    def query_from(i):
        block = (z + nz - i) % nz
        arrived(qbuf.at[c, block], qrecv.at[block])
        share_query(block)

    mine = qbuf.at[c, z]
    for i in NEAR_FIRST:
        go(remote(mine, mine, qsend.at[i], qrecv.at[z], seq_at(z + i, y, c)))

    def pages_of(ref, owner, ch):
        return ref.at[owner, pl.ds(ch * CHUNK, CHUNK)]

    for first, second in ((True, False), (False, True)):
        for ch in range(NCH):
            for is_k, device, way in ((first, yup, 0), (second, ydown, 1)):
                buf, ss, rs = (kbuf, ksend, krecv) if is_k else (vbuf, vsend, vrecv)
                ref = pages_of(buf, y, ch)
                go(remote(ref, ref, ss.at[way, ch], rs.at[y, ch], device))
    for i in (2, 1, 3):
        target = (x + i) % TP
        go(remote(kvpart.at[target], kvin.at[x], tsend.at[i], trecv.at[x], {"tp": target}))
    share_query(z)
    query_from(1)
    query_from(7)

    total = kvpart[x]
    for i in (1, 3, 2):
        source = (x + i) % TP
        arrived(kvin.at[source], trecv.at[source])
        total = total + kvin[source]
    key, value = total[:, :HD], total[:, HD:]
    rotated = key * cosine + pltpu.roll(key, HD // 2, 1) * sine
    fresh = jnp.concatenate([rotated, value], axis=1)
    pages_ref[...] = fresh.astype(BF)
    win[2, y] = jnp.concatenate([fresh, jnp.zeros((TW - T, 2 * HD), F32)], axis=0).astype(BF)
    mine = win.at[2, y]
    go(remote(mine, mine, winsend.at[0], winrecv.at[y], yup))
    go(remote(mine, mine, winsend.at[1], winrecv.at[y], ydown))
    go(remote(mine, mine, winsend.at[2], winrecv.at[y], yfar))

    def forward_pages(ch):
        for buf, ss, rs, owner_y, device in (
            (kbuf, ksend, krecv, yd, yup),
            (vbuf, vsend, vrecv, yu, ydown),
        ):
            ref = pages_of(buf, owner_y, ch)
            arrived(ref, rs.at[owner_y, ch])
            go(remote(ref, ref, ss.at[2, ch], rs.at[owner_y, ch], device))

    query_from(2)
    query_from(6)
    forward_pages(0)
    query_from(3)
    query_from(5)
    forward_pages(1)

    for source in (yu, yd, yf):
        arrived(win.at[2, source], winrecv.at[source])
    go(remote(win.at[2], win.at[1], winsend.at[3], winrecv.at[NY], zup))
    query_from(4)

    for i in range(nz):
        arrived(qbuf.at[1 - c, i], q2recv.at[i])
    half_rows = HEADS * nz * T // 2
    for h in range(2):
        for p in range(2):
            for a in range(HEADS):
                for g in range(GROUPS):
                    pair = [
                        qbuf[g, (z + HALVES[h][2 * p + i]) % nz, :, a * HD : (a + 1) * HD].astype(F32)
                        for i in range(2)
                    ]
                    qc[pl.ds(h * half_rows + a * 4 * T + p * 2 * T, 2 * T), g * HD : (g + 1) * HD] = (
                        jnp.concatenate(pair, axis=0).astype(BF)
                    )

    def prepare(owner_y, ch, slot):
        for j in range(CHUNK):
            page = ch * CHUNK + j
            gate = gmat[pl.ds(owner_y * PAGES + page, 1), :]
            g1 = gate[:, :HD]
            keys = kbuf[owner_y, page].astype(F32)
            kp[slot, j * PAGE : (j + 1) * PAGE, :] = jnp.concatenate(
                [keys * (1.0 - g1), keys * g1], axis=1
            ).astype(BF)
            vals = vbuf[owner_y, page].astype(F32).T
            vt[slot, :HD, j * PAGE : (j + 1) * PAGE] = (vals * (1.0 - g1)).astype(BF)
            vt[slot, HD:, j * PAGE : (j + 1) * PAGE] = (vals * g1).astype(BF)

    def attend(owner_y, ch, slot, rows):
        first_page = owner_y * PAGES + ch * CHUNK
        gates = [gmat[pl.ds(first_page + j, 1), :] > 0.5 for j in range(CHUNK)]
        for r in rows:
            scores = lax.dot_general(
                kp[slot], qc[r * 256 : (r + 1) * 256, :], NT, preferred_element_type=F32
            )
            parts = [scores[j * PAGE : (j + 1) * PAGE, :] * SCALE2 for j in range(CHUNK)]
            old0, old1 = stat[r, 0:1, :], stat[r, 1:2, :]
            new0, new1 = old0, old1
            for j in range(CHUNK):
                top = jnp.max(parts[j], axis=0, keepdims=True)
                new0 = jnp.maximum(new0, jnp.where(gates[j], NEG, top))
                new1 = jnp.maximum(new1, jnp.where(gates[j], top, NEG))
            fall0, fall1 = jnp.exp2(old0 - new0), jnp.exp2(old1 - new1)
            sum0, sum1 = stat[r, 2:3, :] * fall0, stat[r, 3:4, :] * fall1
            weights = []
            for j in range(CHUNK):
                w = jnp.exp2(parts[j] - jnp.where(gates[j], new1, new0))
                row = jnp.sum(w, axis=0, keepdims=True)
                sum0 = sum0 + jnp.where(gates[j], 0.0, row)
                sum1 = sum1 + jnp.where(gates[j], row, 0.0)
                weights.append(w.astype(BF))
            mixed = jnp.dot(
                vt[slot], jnp.concatenate(weights, axis=0), preferred_element_type=F32
            )
            acc[r, :HD, :] = acc[r, :HD, :] * fall0 + mixed[:HD]
            acc[r, HD:, :] = acc[r, HD:, :] * fall1 + mixed[HD:]
            stat[r, 0:1, :] = new0
            stat[r, 1:2, :] = new1
            stat[r, 2:3, :] = sum0
            stat[r, 3:4, :] = sum1

    def step(i, carry):
        turn, ch = i // NCH, i % NCH
        owner_y = (y + turn + turn // 2) % NY

        @pl.when(turn == 1)
        def _():
            arrived(pages_of(kbuf, yu, ch), krecv.at[yu, ch])

        @pl.when(turn == 2)
        def _():
            arrived(pages_of(vbuf, yd, ch), vrecv.at[yd, ch])

        prepare(owner_y, ch, 0)
        attend(owner_y, ch, 0, range(tiles))
        return carry

    def suffix():
        arrived(win.at[0], winrecv.at[NY + 1])
        count = 3 * NY * TW
        key_lane = lane_iota((T, count))
        key_z = z - 2 + key_lane // (NY * TW)
        key_place = (key_z * NY + key_lane // TW % NY) * T + key_lane % TW
        seen = (
            (key_lane % TW < T) & (key_place >= 0) & (key_place <= place)
            & (key_place >= place - offset)
        )
        rows = [win[r, b] for r in range(3) for b in range(NY)]
        keys = jnp.concatenate([b[:, :HD] for b in rows], axis=0)
        vals = jnp.concatenate([b[:, HD:] for b in rows], axis=0)
        lse = jnp.zeros((T, HD), F32)
        for a in range(HEADS):
            sc = lax.dot_general(
                q_ref[:, a * HD : (a + 1) * HD], keys, NT, preferred_element_type=F32
            )
            sc = jnp.where(seen, sc * SCALE2, NEG)
            top = jnp.max(sc, axis=1, keepdims=True)
            w = jnp.where(seen, jnp.exp2(sc - top), 0.0)
            tot = jnp.sum(w, axis=1, keepdims=True)
            out = jnp.dot(w.astype(BF), vals, preferred_element_type=F32)
            osuf[:, a * HD : (a + 1) * HD] = out / tot
            lse = jnp.where(lane_iota((T, HD)) == a, top + jnp.log(tot) * LOG2E, lse)
        lsuf[...] = lse

    lax.fori_loop(0, NCH, step, 0)
    arrived(win.at[1], winrecv.at[NY])
    go(remote(win.at[1], win.at[0], winsend.at[4], winrecv.at[NY + 1], zup))
    lax.fori_loop(NCH, 3 * NCH, step, 0)

    lane = lane_iota((T, HD))

    def build(h, i, g):
        block = HALVES[h][i]
        lse = jnp.zeros((T, HD), F32)
        for a in range(HEADS):
            rows = pl.ds(h * half_rows + a * 4 * T + i * T, T)
            msgs[g, block, :, a * HD : (a + 1) * HD] = ot[rows, g * HD : (g + 1) * HD].astype(BF)
            col = jnp.broadcast_to(st[rows, g : g + 1], (T, HD))
            lse = jnp.where(lane == a, col, lse)
        msgs[g, block, :, HEADS * HD :] = packed_lse(lse)

    def finish(h):
        for r in range(h * tiles // 2, (h + 1) * tiles // 2):
            rows = pl.ds(r * 256, 256)
            s0, s1 = stat[r, 2:3, :], stat[r, 3:4, :]
            ok0, ok1 = s0 > 0.0, s1 > 0.0
            safe0, safe1 = jnp.where(ok0, s0, 1.0), jnp.where(ok1, s1, 1.0)
            inv0, inv1 = 1.0 / safe0, 1.0 / safe1
            lse0 = jnp.where(ok0, stat[r, 0:1, :] + jnp.log(safe0) * LOG2E, NEG)
            lse1 = jnp.where(ok1, stat[r, 1:2, :] + jnp.log(safe1) * LOG2E, NEG)
            ot[rows, :HD] = (acc[r, :HD, :] * inv0).T
            ot[rows, HD:] = (acc[r, HD:, :] * inv1).T
            st[rows, :] = jnp.where(row_iota((HD, 256)) == 0, lse0, lse1).T
        for i in range(4):
            for g in range(GROUPS):
                build(h, i, g)
        for i in range(4):
            block = HALVES[h][i]
            ref = msgs.at[1 - c, block]
            go(remote(ref, half.at[block], hsend.at[block], hrecv.at[block], other))

    def send_half(h):
        for i in range(4):
            block = HALVES[h][i]
            arrived(half.at[block], hrecv.at[block])
            merge_messages([msgs[c, block], half[block]], outbox.at[block])
            if block:
                go(
                    remote(
                        outbox.at[block],
                        inbox.at[block],
                        isend.at[block],
                        irecv.at[block],
                        seq_at(z + block, y, c),
                    )
                )

    for ch in range(NCH):
        arrived(pages_of(kbuf, yf, ch), krecv.at[yf, ch])
        arrived(pages_of(vbuf, yf, ch), vrecv.at[yf, ch])
        prepare(yf, ch, ch)
    for h in range(2):
        for ch in range(NCH):
            attend(yf, ch, ch, range(h * tiles // 2, (h + 1) * tiles // 2))
        if h:
            send_half(0)
        finish(h)
    send_half(1)
    suffix()

    def gather(blocks, store, narrow):
        messages = [inbox[i] for i in blocks]
        if narrow:
            messages.append(outbox[0])
        lses = [unpacked_lse(m[:, HEADS * HD :]) for m in messages] + [lsuf[...]]
        top, total, fractions = shares(lses)
        parts = [head_of(m) for m in messages]
        parts.append(lambda a: osuf[:, a * HD : (a + 1) * HD])
        for a in range(HEADS):
            out = merged_head(parts, fractions, a)
            store[:, a * HD : (a + 1) * HD] = out.astype(store.dtype)
        if narrow:
            lsuf[...] = top + jnp.log(total) * LOG2E

    for i in NEAR_FIRST[:4]:
        arrived(inbox.at[i], irecv.at[i])
    gather(NEAR_FIRST[:4], osuf, True)
    for i in NEAR_FIRST[4:]:
        arrived(inbox.at[i], irecv.at[i])
    gather(NEAR_FIRST[4:], att, False)

    for i in range(TP):
        load_ow[i].wait()
        partial = jnp.dot(att[...], ow[i], preferred_element_type=F32)
        if i < TP - 1:
            target = (x + (2, 1, 3)[i]) % TP
            osend[i] = partial.astype(BF)
            go(remote(osend.at[i], oin.at[x], osendsem.at[i], orecvsem.at[x], {"tp": target}))
        else:
            oown[...] = partial
    total = oown[...]
    for i in (1, 3, 2):
        source = (x + i) % TP
        arrived(oin.at[source], orecvsem.at[source])
        total = total + oin[source].astype(F32)
    hidden_ref[...] = total.astype(BF)

    for copy in sent:
        copy.wait_send()


def local(
    hidden_in, kv_weight, queries, prefix_keys, prefix_values, page_table, suffix_lengths, out_weight
):
    nz = lax.axis_size("seq") // (2 * NY)
    tiles = HEADS * nz * T // 256
    rows = HEADS * nz * T
    exponent = np.tile(np.arange(HD // 2) * 2.0 / HD, 2)
    freq = (500000.0 ** -exponent).astype(np.float32).reshape(1, HD)
    vmem = pl.BlockSpec(memory_space=pltpu.VMEM)
    anywhere = pl.BlockSpec(memory_space=pl.ANY)
    smem = pl.BlockSpec(memory_space=pltpu.SMEM)
    dma = pltpu.SemaphoreType.DMA
    pages = (NY, PAGES, PAGE, HD)
    scratch = [
        pltpu.VMEM((2048, 1024), BF),
        pltpu.VMEM((TP, 1024, 1024), BF),
        pltpu.VMEM(pages, BF),
        pltpu.VMEM(pages, BF),
        pltpu.VMEM((GROUPS, nz, T, HEADS * HD), BF),
        pltpu.VMEM((rows, GROUPS * HD), BF),
        pltpu.VMEM((NY * PAGES, 256), F32),
        pltpu.VMEM((NCH, CK, GROUPS * HD), BF),
        pltpu.VMEM((NCH, GROUPS * HD, CK), BF),
        pltpu.VMEM((tiles, GROUPS * HD, 256), F32),
        pltpu.VMEM((tiles, 8, 256), F32),
        pltpu.VMEM((rows, GROUPS * HD), F32),
        pltpu.VMEM((rows, HD), F32),
        pltpu.VMEM((GROUPS, nz, T, MSG), BF),
        pltpu.VMEM((nz, T, MSG), BF),
        pltpu.VMEM((nz, T, MSG), BF),
        pltpu.VMEM((nz, T, MSG), BF),
        pltpu.VMEM((TP, T, 2 * HD), F32),
        pltpu.VMEM((TP, T, 2 * HD), F32),
        pltpu.VMEM((3, NY, TW, 2 * HD), BF),
        pltpu.VMEM((T, HEADS * HD), F32),
        pltpu.VMEM((T, HD), F32),
        pltpu.VMEM((T, HEADS * HD), BF),
        pltpu.VMEM((T, 1024), F32),
        pltpu.VMEM((TP - 1, T, 1024), BF),
        pltpu.VMEM((TP, T, 1024), BF),
        dma((TP,)),
        dma((3, NCH)),
        dma((3, NCH)),
        dma((NY, NCH)),
        dma((NY, NCH)),
        dma((nz,)),
        dma((nz,)),
        dma((nz,)),
        dma((nz,)),
        dma((TP,)),
        dma((TP,)),
        dma((5,)),
        dma((NY + 2,)),
        dma((nz,)),
        dma((nz,)),
        dma((nz,)),
        dma((nz,)),
        dma((TP,)),
        dma((TP,)),
        dma((4,)),
    ]
    return pl.pallas_call(
        functools.partial(kernel, nz),
        out_shape=(
            jax.ShapeDtypeStruct((T, 1024), BF),
            jax.ShapeDtypeStruct((T, 2 * HD), BF),
        ),
        in_specs=[vmem, anywhere, vmem, anywhere, anywhere, vmem, smem, vmem, anywhere],
        out_specs=(vmem, vmem),
        scratch_shapes=scratch,
        compiler_params=pltpu.CompilerParams(
            collective_id=0, has_side_effects=True, vmem_limit_bytes=56 * 1024 * 1024
        ),
    )(
        hidden_in,
        kv_weight,
        queries,
        prefix_keys,
        prefix_values,
        page_table.reshape(1, -1),
        suffix_lengths,
        freq,
        out_weight,
    )


def solution(mesh):
    return jax.shard_map(
        local,
        mesh=mesh,
        in_specs=(
            P("seq", "tp"),
            P("tp", None),
            P("seq", "tp"),
            P("seq", None, "tp"),
            P("seq", None, "tp"),
            P(),
            P(),
            P("tp", None),
        ),
        out_specs=(P("seq", "tp"), P("seq", "tp")),
        check_vma=False,
    )
```
